1024 devices in a mesh: theta: 64 (over z, y_lo, core), ax: 16 (over y_hi, x).
Axes of the slice: x: 4, y: 8 (y_hi: 4, y_lo: 2; y = y_hi * 2 + y_lo), z: 16, core: 2. Of those that a mesh axis runs over, the one named last changes fastest.
Arguments:
- adjoint_start: float32 [2, 5, 256, 128, 128], P(None, None, 'theta', 'ax'), may hold values from -6 to 6
- jacobian: bfloat16 [7, 5, 5, 256, 128, 128], P(None, None, None, 'theta', 'ax'), may hold values from -1 to 1
- objective_gradient: float32 [2, 5, 256, 128, 128], P(None, None, 'theta', 'ax'), may hold values from -6 to 6
- wall_mask: int32 [256, 128, 128], P('theta', 'ax'), may hold values 0 or 1
Outputs:
- adjoint_end: float32 [2, 5, 256, 128, 128], P(None, None, 'theta', 'ax')
The draws below stay inside these ranges and needn't reach their ends.
All inputs are finite; a program needn't handle non-finite values. No bound on the sum of `wall_mask` on one device may be relied on, other than what follows from the above.
Results may differ from the reference program's by a relative error of at most 0.0003.
Values sent between devices are 32-bit elements; how exact they have to be, the bound alone decides.
A program may use at most 32 MiB of HBM per device.

```python
import jax
import jax.numpy as jnp
from jax import lax

COMP = 5
OBJ = 2
OFFS = 7
SWEEPS = 3
NT = 256
NA = 128
NR = 128


def place_ends(result, stream_key, least, largest):
    shape = result.shape
    spot = [jax.random.randint(jax.random.fold_in(stream_key, axis), (), 0, shape[axis]) for axis in range(len(shape))]
    result = result.at[tuple(spot)].set(least)
    longest = shape.index(max(shape))
    spot[longest] = (spot[longest] + 1) % shape[longest]
    return result.at[tuple(spot)].set(largest)


def steps_of(key, extent, shards, low, high):
    def one(dim, parts):
        draws = jax.random.uniform(jax.random.fold_in(jax.random.fold_in(key, 6), dim), (parts,), jnp.float32, low / len(shards), high / len(shards))
        return jnp.repeat(jnp.exp(draws), extent[dim] // parts).reshape((-1,) + (1,) * (len(extent) - dim - 1))

    gain = one(*shards[0])
    for cut in shards[1:]:
        gain = gain * one(*cut)
    return gain


def gaussian(stream_key, shape, width, most, pieces=(), held_as=jnp.bfloat16):
    entries = width * jax.random.normal(stream_key, shape, jnp.float32)
    if pieces:
        entries = entries * steps_of(stream_key, shape, pieces, -0.22, 0.18)
    return jnp.clip(entries, -most, most).astype(held_as)


def setup_inputs(seed: int = 0) -> dict:
    keys = jax.random.split(jax.random.key(seed), 5)
    adjoint_start = gaussian(keys[0], (OBJ, COMP, NT, NA, NR), 1.0, 6.0, ((2, 64), (3, 16)), jnp.float32)
    jacobian = gaussian(keys[1], (OFFS, COMP, COMP, NT, NA, NR), 35 ** -0.5, 1.0, ((3, 64), (4, 16)))
    objective_gradient = gaussian(keys[2], (OBJ, COMP, NT, NA, NR), 1.0, 6.0, ((2, 64), (3, 16)), jnp.float32)
    wall_mask = place_ends((jax.random.randint(keys[3], (NT, NA, NR), 0, 8) < 1).astype(jnp.int32), jax.random.fold_in(keys[3], 1), 0, 1)
    return {"adjoint_start": adjoint_start, "jacobian": jacobian, "objective_gradient": objective_gradient, "wall_mask": wall_mask}


step_size = 0.4
epsilon = 1e-06

def residual_of(adjoint, jacobian, objective_gradient, wall_mask):
    padded = jnp.pad(adjoint, ((0, 0), (0, 0), (0, 0), (1, 1), (0, 0)))
    neighbours = [adjoint, jnp.roll(adjoint, 1, 2), jnp.roll(adjoint, -1, 2), jnp.roll(adjoint, 2, 2), jnp.roll(adjoint, -2, 2), padded[:, :, :, :-2], padded[:, :, :, 2:]]
    summed = -objective_gradient
    for offset in range(7):
        summed = summed + jnp.einsum('mnabc,jmabc->jnabc', jacobian[offset].astype(jnp.float32), neighbours[offset], precision=lax.Precision.HIGHEST)
    return jnp.where(wall_mask[None, None] == 1, jnp.float32(0.0), summed)

def reference(adjoint_start, jacobian, objective_gradient, wall_mask):
    adjoint = adjoint_start
    cells = adjoint.shape[1] * adjoint.shape[2] * adjoint.shape[3] * adjoint.shape[4]
    for sweep_index in range(SWEEPS):
        summed = residual_of(adjoint, jacobian, objective_gradient, wall_mask)
        squares = lax.optimization_barrier(jnp.sum(summed * summed, axis=(1, 2, 3, 4)))
        norm_value = jnp.sqrt(squares / cells + epsilon)
        adjoint = adjoint - step_size * summed / norm_value[:, None, None, None, None]
    return adjoint
```

```python
import functools

import jax
import jax.numpy as jnp
from jax import lax
from jax.experimental import pallas as pl
from jax.experimental.pallas import tpu as pltpu
from jax.sharding import PartitionSpec as P

MESH = pl.DeviceIdType.MESH
F32 = jnp.float32
SWEEPS = 3
OBJ = 2
COMP = 5
NT = 4
STEP = 0.4
EPS = 1e-06
SHIFT = (0, -1, 1, -2, 2)

X = 4
YL = 2
CORES = 2


def near_last(size):
    return sorted(range(1, size), key=lambda d: -min(d, size - d))


def peer(n_theta, n_ax, dx=0, dy=0, dz=0, dc=0):
    theta, ax = lax.axis_index("theta"), lax.axis_index("ax")
    nz, ny = n_theta // (YL * CORES), (n_ax // X) * YL
    if dz:
        theta = (theta + YL * CORES * dz) % n_theta
    if dx:
        ax = (ax // X) * X + (ax % X + dx) % X
    if dc:
        theta = (theta // CORES) * CORES + (theta % CORES + dc) % CORES
    if dy:
        y_lo = (theta // CORES) % YL
        y = ((ax // X) * YL + y_lo + dy) % ny
        ax = (y // YL) * X + ax % X
        theta = theta + (y % YL - y_lo) * CORES
    return theta, ax


def stages(n_theta, n_ax):
    nz, ny = n_theta // (YL * CORES), (n_ax // X) * YL
    pairs = [(dx, dc) for dx in range(X) for dc in range(CORES) if dx or dc]
    pairs.sort(key=lambda p: (-min(p[0], X - p[0]), p[1]))
    return (
        [dict(dx=dx, dc=dc) for dx, dc in pairs],
        [dict(dy=dy) for dy in near_last(ny)],
        [dict(dz=dz) for dz in near_last(nz)],
    )


def two_sum(a, b):
    s = a + b
    bb = s - a
    return s, (a - (s - bb)) + (b - bb)


def fast_two_sum(a, b):
    s = a + b
    return s, b - (s - a)


def split(a):
    c = a * F32(4097.0)
    hi = c - (c - a)
    return hi, a - hi


def two_prod(a, sa, b, sb):
    p = a * b
    return p, ((sa[0] * sb[0] - p) + sa[0] * sb[1] + sa[1] * sb[0]) + sa[1] * sb[1]


def pair_add(a, b):
    s, e = two_sum(a[0], b[0])
    return s, e + (a[1] + b[1])


def norm_pair(a):
    return fast_two_sum(a[0], a[1])


def pair_mul(a, b):
    p, e = two_prod(a[0], split(a[0]), b[0], split(b[0]))
    return fast_two_sum(p, e + (a[0] * b[1] + a[1] * b[0]))


def scaled(a, k):
    return a[0] * F32(k), a[1] * F32(k)


def roll(x, shift, axis):
    return pltpu.roll(x, shift % x.shape[axis], axis)


def fold_rows(parts, sub):
    for k in (4, 2, 1):
        half = len(parts) // 2
        first = (sub // k) % 2 == 0
        merged = []
        for i in range(half):
            a, b = parts[i], parts[i + half]
            low = tuple(jnp.where(first, u, roll(v, k, 0)) for u, v in zip(a, b))
            high = tuple(jnp.where(first, roll(u, 8 - k, 0), v) for u, v in zip(a, b))
            merged.append(pair_add(low, high))
        parts = merged
    return parts[0]


def fold_lanes(part):
    for k in (64, 32, 16, 8, 4, 2, 1):
        part = pair_add(part, tuple(roll(v, k, 1) for v in part))
    return norm_pair(part)


def kernel(n_theta, n_ax, a_hbm, j_hbm, g_hbm, w_hbm, out_ref,
           fld, axs, axh, jb, jf, gb, wb, early, msg, got0, got1, got2,
           in_sem, send_sem, recv_sem, ar_send, ar_recv):
    theta, ax = lax.axis_index("theta"), lax.axis_index("ax")
    around = [
        ((theta + n_theta - 1) % n_theta, ax),
        ((theta + 1) % n_theta, ax),
        (theta, (ax + n_ax - 1) % n_ax),
        (theta, (ax + 1) % n_ax),
    ]
    levels = stages(n_theta, n_ax)
    barrier = pltpu.get_barrier_semaphore()
    greeted = around + [peer(n_theta, n_ax, **p) for level in reversed(levels) for p in level]
    for dev in greeted:
        pl.semaphore_signal(barrier, inc=1, device_id=dev, device_id_type=MESH)

    loads = [
        pltpu.make_async_copy(j_hbm, jb, in_sem.at[0]),
        pltpu.make_async_copy(a_hbm, fld.at[0, :, :, 2:6], in_sem.at[1]),
        pltpu.make_async_copy(g_hbm, gb, in_sem.at[2]),
        pltpu.make_async_copy(w_hbm, wb, in_sem.at[3]),
    ]
    for load in loads:
        load.start()

    sub = lax.broadcasted_iota(jnp.int32, (8, 128), 0)
    lane = lax.broadcasted_iota(jnp.int32, (8, 128), 1)
    sub3 = lax.broadcasted_iota(jnp.int32, (OBJ, 8, 128), 1)

    def put_rows(slot, t, value):
        axs[slot, 0, :, :, t] = value[:, :, 0:1, :]
        axs[slot, 1, :, :, t] = value[:, :, 7:8, :]

    def halo_copies(slot):
        moves = (
            (fld.at[slot, :, :, 2:4], fld.at[slot, :, :, 6:8]),
            (fld.at[slot, :, :, 4:6], fld.at[slot, :, :, 0:2]),
            (axs.at[slot, 0], axh.at[slot, 1]),
            (axs.at[slot, 1], axh.at[slot, 0]),
        )
        return [
            pltpu.make_async_remote_copy(
                src_ref=src, dst_ref=dst, send_sem=send_sem.at[slot, i], recv_sem=recv_sem.at[slot, i],
                device_id=around[i], device_id_type=MESH)
            for i, (src, dst) in enumerate(moves)
        ]

    def local(slot, t):
        if slot == 0:
            acc = -gb[:, :, t]
        else:
            acc = jnp.zeros((OBJ, COMP, 8, 128), F32)
        for o in range(5):
            if 0 <= t + SHIFT[o] < NT:
                for m in range(COMP):
                    near = fld[slot, :, m, 2 + t + SHIFT[o]]
                    acc = acc + jf[o, m, :, t][None] * near[:, None]
        fld[slot + 1, :, :, 2 + t] = acc

    def rest(slot, t):
        acc = fld[slot + 1, :, :, 2 + t]
        for o in range(5):
            if not 0 <= t + SHIFT[o] < NT:
                for m in range(COMP):
                    near = fld[slot, :, m, 2 + t + SHIFT[o]]
                    acc = acc + jf[o, m, :, t][None] * near[:, None]
        for m in range(COMP):
            here = fld[slot, :, m, 2 + t]
            low, high = axh[slot, 0, :, m, t], axh[slot, 1, :, m, t]
            low = jnp.where(ax == 0, F32(0.0), low)
            high = jnp.where(ax == n_ax - 1, F32(0.0), high)
            below = jnp.where(sub3 == 0, low, pltpu.roll(here, 1, 1))
            above = jnp.where(sub3 == 7, high, pltpu.roll(here, 7, 1))
            acc = acc + jf[5, m, :, t][None] * below[:, None]
            acc = acc + jf[6, m, :, t][None] * above[:, None]
        acc = jnp.where(wb[t] == 1, F32(0.0), acc)
        fld[slot + 1, :, :, 2 + t] = acc
        if slot + 1 < SWEEPS:
            put_rows(slot + 1, t, acc)

    def products(wanted):
        names = sorted({s for pair in wanted for s in pair})

        def body(n, sums):
            sums = list(sums)
            for t in range(NT):
                values = {s: fld[s, :, n, 2 + t] for s in names}
                halves = {s: split(values[s]) for s in names}
                for i, (a, b) in enumerate(wanted):
                    p, e = two_prod(values[a], halves[a], values[b], halves[b])
                    s, d = two_sum(sums[i][0], p)
                    sums[i] = (s, sums[i][1] + (d + e))
            return tuple(sums)

        zero = jnp.zeros((OBJ, 8, 128), F32)
        sums = lax.fori_loop(0, COMP, body, ((zero, zero),) * len(wanted))
        parts = [tuple(v[j] for v in s) for s in sums for j in range(OBJ)]
        nothing = jnp.zeros((8, 128), F32)
        return fold_lanes(fold_rows(parts + [(nothing, nothing)] * (8 - len(parts)), sub))

    def on_lanes(part, start):
        return (jnp.where(lane == sub + start, part[0], F32(0.0))
                + jnp.where(lane == sub + (start + 8), part[1], F32(0.0)))

    loads[1].wait()
    for t in range(NT):
        put_rows(0, t, fld[0, :, :, 2 + t])
    loads[0].wait()

    def widen(i, carry):
        for m in range(COMP):
            jf[i, m] = jb[i, m].astype(F32)
        return carry

    lax.fori_loop(0, 7, widen, 0)
    loads[2].wait()
    loads[3].wait()
    pl.semaphore_wait(barrier, len(greeted))

    moving = []
    for slot in range(SWEEPS):
        copies = halo_copies(slot)
        for copy in copies:
            copy.start()
        moving += copies
        for t in range(NT):
            local(slot, t)
        if slot == 2:
            early[...] = on_lanes(products([(1, 1), (1, 2), (2, 2)]), 16)
        for copy in copies:
            copy.wait_recv()
        for t in range(NT):
            rest(slot, t)

    row = on_lanes(products([(1, 3), (2, 3), (3, 3)]), 0) + early[...]
    for k in (4, 2, 1):
        row = row + roll(row, k, 0)
    is_value = (lane // 8) % 2 == 0
    for i, (level, got) in enumerate(zip(levels, (got0, got1, got2))):
        msg[i] = row[0:1]
        for k, offset in enumerate(level):
            pltpu.make_async_remote_copy(
                src_ref=msg.at[i], dst_ref=got.at[k], send_sem=ar_send.at[i], recv_sem=ar_recv.at[i],
                device_id=peer(n_theta, n_ax, **offset), device_id_type=MESH).start()
        pltpu.make_async_copy(got, got, ar_recv.at[i]).wait()
        sums = [(row[0:1], jnp.zeros((1, 128), F32))]
        sums += [(got[k], jnp.zeros((1, 128), F32)) for k in range(len(level))]
        while len(sums) > 1:
            paired = [pair_add(a, b) for a, b in zip(sums[0::2], sums[1::2])]
            sums = paired + sums[2 * len(paired):]
        value, error = (jnp.broadcast_to(v, (8, 128)) for v in sums[0])
        value, error = fast_two_sum(value, error + roll(value, -8, 1) + roll(error, -8, 1))
        row = jnp.where(is_value, value, roll(error, 8, 1))

    def gram(start, k):
        place = start + OBJ * k
        return roll(row, -place, 1), roll(row, -place - 8, 1)

    g02, g12, g22 = (gram(0, k) for k in range(3))
    g00, g01, g11 = (gram(16, k) for k in range(3))
    cells = F32(COMP * NT * 8 * 128 * n_theta * n_ax)
    nothing = jnp.zeros((8, 128), F32)

    def step_of(square):
        mean = jnp.maximum(square[0] + square[1], F32(0.0)) / cells
        return F32(STEP) / jnp.sqrt(mean + F32(EPS))

    c0 = step_of(g00)
    p0 = (c0, nothing)
    square1 = pair_add(g00, pair_mul(p0, pair_add(pair_mul(p0, g11), scaled(g01, -2.0))))
    c1 = step_of(square1)
    both = two_sum(c0, c1)
    times = two_prod(c0, split(c0), c1, split(c1))
    inner = pair_add(pair_mul(both, g11), scaled(g01, -2.0))
    outer = pair_add(scaled(pair_add(g02, scaled(pair_mul(both, g12), -1.0)), 2.0), pair_mul(times, g22))
    square2 = pair_add(g00, pair_add(pair_mul(both, inner), pair_mul(times, outer)))
    c2 = step_of(square2)

    def spread(c):
        picked = [jnp.sum(jnp.where(lane == j, c, F32(0.0)), axis=1, keepdims=True) for j in range(OBJ)]
        return jnp.stack([jnp.broadcast_to(v, (8, 128)) for v in picked])[:, None]

    c0, c1, c2 = spread(c0), spread(c1), spread(c2)
    for t in range(NT):
        f0, f1, f2 = (fld[s, :, :, 2 + t] for s in (1, 2, 3))
        r1 = f0 - c0 * f1
        r2 = r1 - c1 * (f1 - c0 * f2)
        out_ref[:, :, t] = c0 * f0 + c1 * r1 + c2 * r2

    for copy in moving:
        copy.wait_send()
    for i, got in enumerate((got0, got1, got2)):
        pltpu.make_async_copy(got, got, ar_send.at[i]).wait()


def per_device(n_theta, n_ax, adjoint_start, jacobian, objective_gradient, wall_mask):
    field = adjoint_start.shape
    levels = stages(n_theta, n_ax)
    update = pl.pallas_call(
        functools.partial(kernel, n_theta, n_ax),
        out_shape=jax.ShapeDtypeStruct(field, F32),
        in_specs=[pl.BlockSpec(memory_space=pl.ANY)] * 4,
        out_specs=pl.BlockSpec(memory_space=pltpu.VMEM),
        scratch_shapes=[
            pltpu.VMEM((SWEEPS + 1, OBJ, COMP, NT + 4, 8, 128), F32),
            pltpu.VMEM((SWEEPS, 2, OBJ, COMP, NT, 1, 128), F32),
            pltpu.VMEM((SWEEPS, 2, OBJ, COMP, NT, 1, 128), F32),
            pltpu.VMEM(jacobian.shape, jnp.bfloat16),
            pltpu.VMEM(jacobian.shape, F32),
            pltpu.VMEM(field, F32),
            pltpu.VMEM(wall_mask.shape, jnp.int32),
            pltpu.VMEM((8, 128), F32),
            pltpu.VMEM((3, 1, 128), F32),
        ]
        + [pltpu.VMEM((len(level), 1, 128), F32) for level in levels]
        + [
            pltpu.SemaphoreType.DMA((4,)),
            pltpu.SemaphoreType.DMA((SWEEPS, 4)),
            pltpu.SemaphoreType.DMA((SWEEPS, 4)),
            pltpu.SemaphoreType.DMA((3,)),
            pltpu.SemaphoreType.DMA((3,)),
        ],
        compiler_params=pltpu.CompilerParams(collective_id=0, has_side_effects=True),
        name="sweeps",
    )(adjoint_start, jacobian, objective_gradient, wall_mask)
    return adjoint_start - update


def solution(mesh):
    placed = (
        P(None, None, "theta", "ax", None),
        P(None, None, None, "theta", "ax", None),
        P(None, None, "theta", "ax", None),
        P("theta", "ax", None),
    )
    return jax.shard_map(
        functools.partial(per_device, mesh.shape["theta"], mesh.shape["ax"]),
        mesh=mesh,
        in_specs=placed,
        out_specs=P(None, None, "theta", "ax", None),
        check_vma=False,
    )
```

```python
import functools

import jax
import jax.numpy as jnp
from jax import lax
from jax.experimental import pallas as pl
from jax.experimental.pallas import tpu as pltpu
from jax.sharding import PartitionSpec as P

MESH = pl.DeviceIdType.MESH
F32 = jnp.float32
SWEEPS = 3
OBJ = 2
COMP = 5
NT = 4
STEP = 0.4
EPS = 1e-06
SHIFT = (0, -1, 1, -2, 2)

X = 4
YL = 2
CORES = 2


def near_last(size):
    return sorted(range(1, size), key=lambda d: -min(d, size - d))


def peer(n_theta, n_ax, dx=0, dy=0, dz=0, dc=0):
    theta, ax = lax.axis_index("theta"), lax.axis_index("ax")
    nz, ny = n_theta // (YL * CORES), (n_ax // X) * YL
    if dz:
        theta = (theta + YL * CORES * dz) % n_theta
    if dx:
        ax = (ax // X) * X + (ax % X + dx) % X
    if dc:
        theta = (theta // CORES) * CORES + (theta % CORES + dc) % CORES
    if dy:
        y_lo = (theta // CORES) % YL
        y = ((ax // X) * YL + y_lo + dy) % ny
        ax = (y // YL) * X + ax % X
        theta = theta + (y % YL - y_lo) * CORES
    return theta, ax


def stages(n_theta, n_ax):
    nz, ny = n_theta // (YL * CORES), (n_ax // X) * YL
    plane = [(dx, dy) for dx in range(X) for dy in range(ny) if dx or dy]
    plane.sort(key=lambda p: -min(p[0], X - p[0]) - min(p[1], ny - p[1]))
    ring = [(dz, dc) for dz in near_last(nz) + [0] for dc in range(CORES) if dz or dc]
    return (
        [dict(dx=dx, dy=dy) for dx, dy in plane],
        [dict(dz=dz, dc=dc) for dz, dc in ring],
    )


def rows_of(level):
    return -(-(len(level) + 1) // 8) * 8


def two_sum(a, b):
    s = a + b
    bb = s - a
    return s, (a - (s - bb)) + (b - bb)


def fast_two_sum(a, b):
    s = a + b
    return s, b - (s - a)


def split(a):
    c = a * F32(4097.0)
    hi = c - (c - a)
    return hi, a - hi


def two_prod(a, sa, b, sb):
    p = a * b
    return p, ((sa[0] * sb[0] - p) + sa[0] * sb[1] + sa[1] * sb[0]) + sa[1] * sb[1]


def pair_add(a, b):
    s, e = two_sum(a[0], b[0])
    return s, e + (a[1] + b[1])


def norm_pair(a):
    return fast_two_sum(a[0], a[1])


def pair_mul(a, b):
    p, e = two_prod(a[0], split(a[0]), b[0], split(b[0]))
    return fast_two_sum(p, e + (a[0] * b[1] + a[1] * b[0]))


def scaled(a, k):
    return a[0] * F32(k), a[1] * F32(k)


def roll(x, shift, axis):
    return pltpu.roll(x, shift % x.shape[axis], axis)


def fold_rows(parts, sub):
    for k in (4, 2, 1):
        half = len(parts) // 2
        first = (sub // k) % 2 == 0
        merged = []
        for i in range(half):
            a, b = parts[i], parts[i + half]
            low = tuple(jnp.where(first, u, roll(v, k, 0)) for u, v in zip(a, b))
            high = tuple(jnp.where(first, roll(u, 8 - k, 0), v) for u, v in zip(a, b))
            merged.append(pair_add(low, high))
        parts = merged
    return parts[0]


def fold_lanes(part):
    for k in (64, 32, 16, 8, 4, 2, 1):
        part = pair_add(part, tuple(roll(v, k, 1) for v in part))
    return norm_pair(part)


def kernel(n_theta, n_ax, a_hbm, j_hbm, g_hbm, w_hbm, out_ref,
           fld, axh, jb, jf, je, gb, wb, early, msg, got0, got1,
           in_sem, send_sem, recv_sem, ar_send, ar_recv, ready):
    theta, ax = lax.axis_index("theta"), lax.axis_index("ax")
    around = [
        ((theta + n_theta - 1) % n_theta, ax),
        ((theta + 1) % n_theta, ax),
        (theta, (ax + n_ax - 1) % n_ax),
        (theta, (ax + 1) % n_ax),
    ]
    levels = stages(n_theta, n_ax)
    barrier = pltpu.get_barrier_semaphore()
    nz, ny = n_theta // (YL * CORES), (n_ax // X) * YL

    def tell(sem, devices):
        for dev in devices:
            pl.semaphore_signal(sem, inc=1, device_id=dev, device_id_type=MESH)

    near = (-3, -2, -1, 1, 2, 3)
    offsets = (
        [dict(dc=1)]
        + [dict(dx=d) for d in range(1, X)]
        + [dict(dy=d) for d in sorted({k % ny for k in near} - {0})]
        + [dict(dz=d) for d in sorted({k % nz for k in near} - {0})]
    )
    two, three = min(2, nz - 1), min(3, nz - 1)
    columns = [dict(dx=d) for d in range(1, X)]
    first = columns + [dict(dc=1), dict(dy=ny - 1), dict(dz=three), dict(dz=nz - three)]
    second = columns + [dict(dz=two), dict(dz=nz - two), dict(dz=three, dc=1), dict(dz=nz - three, dc=1)]
    greeted = around + [peer(n_theta, n_ax, **p) for p in offsets]
    tell(barrier, around)
    for level, got in zip(levels, (got0, got1)):
        if len(level) + 1 < got.shape[0]:
            got[len(level) + 1 :] = jnp.zeros((got.shape[0] - len(level) - 1, 128), F32)

    loads = [
        pltpu.make_async_copy(j_hbm, jb, in_sem.at[0]),
        pltpu.make_async_copy(a_hbm, fld.at[0, :, :, 2:6], in_sem.at[1]),
        pltpu.make_async_copy(g_hbm, gb, in_sem.at[2]),
        pltpu.make_async_copy(w_hbm, wb, in_sem.at[3]),
    ]
    for load in loads:
        load.start()
    tell(barrier, greeted[len(around):])
    pl.semaphore_wait(barrier, len(greeted))

    sub = lax.broadcasted_iota(jnp.int32, (8, 128), 0)
    lane = lax.broadcasted_iota(jnp.int32, (8, 128), 1)
    sub3 = lax.broadcasted_iota(jnp.int32, (OBJ, 8, 128), 1)

    def halo_copies(slot):
        mine = a_hbm if slot == 0 else fld.at[slot, :, :, 2:6]
        moves = (
            (mine.at[:, :, 0:2], fld.at[slot, :, :, 6:8]),
            (mine.at[:, :, 2:4], fld.at[slot, :, :, 0:2]),
            (mine.at[:, :, :, 0:1], axh.at[slot, 1]),
            (mine.at[:, :, :, 7:8], axh.at[slot, 0]),
        )
        return [
            pltpu.make_async_remote_copy(
                src_ref=src, dst_ref=dst, send_sem=send_sem.at[slot, i], recv_sem=recv_sem.at[slot, i],
                device_id=around[i], device_id_type=MESH)
            for i, (src, dst) in enumerate(moves)
        ]

    def theta_part(acc, slot, t, inside):
        for o in range(5):
            if (0 <= t + SHIFT[o] < NT) == inside:
                for m in range(COMP):
                    near = fld[slot, :, m, 2 + t + SHIFT[o]]
                    acc = acc + jf[o, m, :, t][None] * near[:, None]
        return acc

    def local(slot, t):
        acc = -gb[:, :, t] if slot == 0 else jnp.zeros((OBJ, COMP, 8, 128), F32)
        acc = theta_part(acc, slot, t, True)
        for m in range(COMP):
            here = fld[slot, :, m, 2 + t]
            below = jnp.where(sub3 == 0, F32(0.0), pltpu.roll(here, 1, 1))
            above = jnp.where(sub3 == 7, F32(0.0), pltpu.roll(here, 7, 1))
            acc = acc + jf[5, m, :, t][None] * below[:, None]
            acc = acc + jf[6, m, :, t][None] * above[:, None]
        fld[slot + 1, :, :, 2 + t] = acc

    def rest(slot, t):
        acc = theta_part(fld[slot + 1, :, :, 2 + t], slot, t, False)
        for m in range(COMP):
            edge = jnp.where(sub3 < 4, axh[slot, 0, :, m, t], axh[slot, 1, :, m, t])
            acc = acc + je[m, :, t][None] * edge[:, None]
        acc = jnp.where(wb[t] == 1, F32(0.0), acc)
        fld[slot + 1, :, :, 2 + t] = acc
        return acc

    def add_products(sums, values, wanted):
        halves = {s: split(v) for s, v in values.items()}
        sums = list(sums)
        for i, (a, b) in enumerate(wanted):
            p, e = two_prod(values[a], halves[a], values[b], halves[b])
            s, d = two_sum(sums[i][0], p)
            sums[i] = (s, sums[i][1] + (d + e))
        return sums

    zero = jnp.zeros((OBJ, 8, 128), F32)

    def folded(sums):
        parts = [tuple(v[j] for v in s) for s in sums for j in range(OBJ)]
        nothing = jnp.zeros((8, 128), F32)
        return fold_lanes(fold_rows(parts + [(nothing, nothing)] * (8 - len(parts)), sub))

    def early_products(n, sums):
        for t in range(NT):
            values = {s: fld[s, :, n, 2 + t] for s in (1, 2)}
            sums = add_products(sums, values, ((1, 1), (1, 2), (2, 2)))
        return tuple(sums)

    def on_lanes(part, start):
        return (jnp.where(lane == sub + start, part[0], F32(0.0))
                + jnp.where(lane == sub + (start + 8), part[1], F32(0.0)))

    moving = []
    for slot in range(SWEEPS):
        copies = halo_copies(slot)
        for copy in (copies[2], copies[3], copies[0], copies[1]):
            copy.start()
        moving += copies
        if slot == 0:
            tell(ready.at[0], [peer(n_theta, n_ax, **p) for p in first])
            loads[0].wait()

            def widen(i, carry):
                for m in range(COMP):
                    jf[i, m] = jb[i, m].astype(F32)
                return carry

            lax.fori_loop(0, 7, widen, 0)
            low = jnp.where(sub == 0, jnp.where(ax == 0, F32(0.0), F32(1.0)), F32(0.0))
            high = jnp.where(sub == 7, jnp.where(ax == n_ax - 1, F32(0.0), F32(1.0)), F32(0.0))

            def edges(m, carry):
                je[m] = jf[5, m] * low + jf[6, m] * high
                return carry

            lax.fori_loop(0, COMP, edges, 0)
            for load in loads[1:]:
                load.wait()
        for t in range(NT):
            local(slot, t)
        if slot == 2:
            early[...] = on_lanes(folded(lax.fori_loop(0, COMP, early_products, ((zero, zero),) * 3)), 16)
        for copy in copies:
            copy.wait_recv()
        if slot == 1:
            pl.semaphore_wait(ready.at[0], len(first))
            tell(ready.at[1], [peer(n_theta, n_ax, **p) for p in second])
        if slot == 2:
            pl.semaphore_wait(ready.at[1], len(second))
        sums = [(zero, zero)] * 3
        for t in range(NT):
            acc = rest(slot, t)
            if slot == 2:
                for n in range(COMP):
                    values = {1: fld[1, :, n, 2 + t], 2: fld[2, :, n, 2 + t], 3: acc[:, n]}
                    sums = add_products(sums, values, ((1, 3), (2, 3), (3, 3)))

    row = on_lanes(folded(sums), 0) + early[...]
    for k in (4, 2, 1):
        row = row + roll(row, k, 0)
    is_value = (lane // 8) % 2 == 0
    for i, (level, got) in enumerate(zip(levels, (got0, got1))):
        msg[i] = row
        for k, offset in enumerate(level):
            pltpu.make_async_remote_copy(
                src_ref=msg.at[i, 0:1], dst_ref=got.at[k : k + 1], send_sem=ar_send.at[i],
                recv_sem=ar_recv.at[i], device_id=peer(n_theta, n_ax, **offset), device_id_type=MESH).start()
        got[len(level) : len(level) + 1] = row[0:1]
        heard = got.at[0 : len(level)]
        pltpu.make_async_copy(heard, heard, ar_recv.at[i]).wait()
        sums = [(got[k : k + 8], jnp.zeros((8, 128), F32)) for k in range(0, got.shape[0], 8)]
        while len(sums) > 1:
            paired = [pair_add(a, b) for a, b in zip(sums[0::2], sums[1::2])]
            sums = paired + sums[2 * len(paired):]
        value, error = sums[0]
        for k in (4, 2, 1):
            value, error = pair_add((value, error), (roll(value, k, 0), roll(error, k, 0)))
        value, error = fast_two_sum(value, error + roll(value, -8, 1) + roll(error, -8, 1))
        row = jnp.where(is_value, value, roll(error, 8, 1))

    def gram(start, k):
        place = start + OBJ * k
        return roll(row, -place, 1), roll(row, -place - 8, 1)

    g02, g12, g22 = (gram(0, k) for k in range(3))
    g00, g01, g11 = (gram(16, k) for k in range(3))
    cells = F32(COMP * NT * 8 * 128 * n_theta * n_ax)
    nothing = jnp.zeros((8, 128), F32)

    def step_of(square):
        mean = jnp.maximum(square[0] + square[1], F32(0.0)) / cells
        return F32(STEP) / jnp.sqrt(mean + F32(EPS))

    c0 = step_of(g00)
    p0 = (c0, nothing)
    square1 = pair_add(g00, pair_mul(p0, pair_add(pair_mul(p0, g11), scaled(g01, -2.0))))
    c1 = step_of(square1)
    both = two_sum(c0, c1)
    times = two_prod(c0, split(c0), c1, split(c1))
    inner = pair_add(pair_mul(both, g11), scaled(g01, -2.0))
    outer = pair_add(scaled(pair_add(g02, scaled(pair_mul(both, g12), -1.0)), 2.0), pair_mul(times, g22))
    square2 = pair_add(g00, pair_add(pair_mul(both, inner), pair_mul(times, outer)))
    c2 = step_of(square2)

    def spread(c):
        picked = [jnp.sum(jnp.where(lane == j, c, F32(0.0)), axis=1, keepdims=True) for j in range(OBJ)]
        return jnp.stack([jnp.broadcast_to(v, (8, 128)) for v in picked])[:, None]

    c0, c1, c2 = spread(c0), spread(c1), spread(c2)
    for t in range(NT):
        f0, f1, f2 = (fld[s, :, :, 2 + t] for s in (1, 2, 3))
        r1 = f0 - c0 * f1
        r2 = r1 - c1 * (f1 - c0 * f2)
        out_ref[:, :, t] = c0 * f0 + c1 * r1 + c2 * r2

    for copy in moving:
        copy.wait_send()
    for i, got in enumerate((got0, got1)):
        heard = got.at[0 : len(levels[i])]
        pltpu.make_async_copy(heard, heard, ar_send.at[i]).wait()


def per_device(n_theta, n_ax, adjoint_start, jacobian, objective_gradient, wall_mask):
    field = adjoint_start.shape
    levels = stages(n_theta, n_ax)
    update = pl.pallas_call(
        functools.partial(kernel, n_theta, n_ax),
        out_shape=pltpu.VMEM(field, F32),
        in_specs=[pl.BlockSpec(memory_space=pl.ANY)] * 4,
        out_specs=pl.BlockSpec(memory_space=pltpu.VMEM),
        scratch_shapes=[
            pltpu.VMEM((SWEEPS + 1, OBJ, COMP, NT + 4, 8, 128), F32),
            pltpu.VMEM((SWEEPS, 2, OBJ, COMP, NT, 1, 128), F32),
            pltpu.VMEM(jacobian.shape, jnp.bfloat16),
            pltpu.VMEM(jacobian.shape, F32),
            pltpu.VMEM((COMP, COMP, NT, 8, 128), F32),
            pltpu.VMEM(field, F32),
            pltpu.VMEM(wall_mask.shape, jnp.int32),
            pltpu.VMEM((8, 128), F32),
            pltpu.VMEM((2, 8, 128), F32),
        ]
        + [pltpu.VMEM((rows_of(level), 128), F32) for level in levels]
        + [
            pltpu.SemaphoreType.DMA((4,)),
            pltpu.SemaphoreType.DMA((SWEEPS, 4)),
            pltpu.SemaphoreType.DMA((SWEEPS, 4)),
            pltpu.SemaphoreType.DMA((2,)),
            pltpu.SemaphoreType.DMA((2,)),
            pltpu.SemaphoreType.REGULAR((2,)),
        ],
        compiler_params=pltpu.CompilerParams(collective_id=0, has_side_effects=True),
        name="sweeps",
    )(adjoint_start, jacobian, objective_gradient, wall_mask)
    return adjoint_start - update


def solution(mesh):
    placed = (
        P(None, None, "theta", "ax", None),
        P(None, None, None, "theta", "ax", None),
        P(None, None, "theta", "ax", None),
        P("theta", "ax", None),
    )
    return jax.shard_map(
        functools.partial(per_device, mesh.shape["theta"], mesh.shape["ax"]),
        mesh=mesh,
        in_specs=placed,
        out_specs=P(None, None, "theta", "ax", None),
        check_vma=False,
    )
```

```python
import functools

import jax
import jax.numpy as jnp
from jax import lax
from jax.experimental import pallas as pl
from jax.experimental.pallas import tpu as pltpu
from jax.sharding import PartitionSpec as P

MESH = pl.DeviceIdType.MESH
F32 = jnp.float32
SWEEPS = 3
OBJ = 2
COMP = 5
NT = 4
STEP = 0.4
EPS = 1e-06
SHIFT = (0, -1, 1, -2, 2)

X = 4
YL = 2
CORES = 2


def near_last(size):
    return sorted(range(1, size), key=lambda d: -min(d, size - d))


def peer(n_theta, n_ax, dx=0, dy=0, dz=0, dc=0):
    theta, ax = lax.axis_index("theta"), lax.axis_index("ax")
    nz, ny = n_theta // (YL * CORES), (n_ax // X) * YL
    if dz:
        theta = (theta + YL * CORES * dz) % n_theta
    if dx:
        ax = (ax // X) * X + (ax % X + dx) % X
    if dc:
        theta = (theta // CORES) * CORES + (theta % CORES + dc) % CORES
    if dy:
        y_lo = (theta // CORES) % YL
        y = ((ax // X) * YL + y_lo + dy) % ny
        ax = (y // YL) * X + ax % X
        theta = theta + (y % YL - y_lo) * CORES
    return theta, ax


def stages(n_theta, n_ax):
    nz, ny = n_theta // (YL * CORES), (n_ax // X) * YL
    plane = [(dx, dy) for dx in range(X) for dy in range(ny) if dx or dy]
    plane.sort(key=lambda p: -min(p[0], X - p[0]) - min(p[1], ny - p[1]))
    ring = [(dz, dc) for dz in near_last(nz) + [0] for dc in range(CORES) if dz or dc]
    return (
        [dict(dx=dx, dy=dy) for dx, dy in plane],
        [dict(dz=dz, dc=dc) for dz, dc in ring],
    )


def rows_of(level):
    return -(-(len(level) + 1) // 8) * 8


def two_sum(a, b):
    s = a + b
    bb = s - a
    return s, (a - (s - bb)) + (b - bb)


def fast_two_sum(a, b):
    s = a + b
    return s, b - (s - a)


def split(a):
    c = a * F32(4097.0)
    hi = c - (c - a)
    return hi, a - hi


def two_prod(a, sa, b, sb):
    p = a * b
    return p, ((sa[0] * sb[0] - p) + sa[0] * sb[1] + sa[1] * sb[0]) + sa[1] * sb[1]


def pair_add(a, b):
    s, e = two_sum(a[0], b[0])
    return s, e + (a[1] + b[1])


def norm_pair(a):
    return fast_two_sum(a[0], a[1])


def pair_mul(a, b):
    p, e = two_prod(a[0], split(a[0]), b[0], split(b[0]))
    return fast_two_sum(p, e + (a[0] * b[1] + a[1] * b[0]))


def scaled(a, k):
    return a[0] * F32(k), a[1] * F32(k)


def roll(x, shift, axis):
    return pltpu.roll(x, shift % x.shape[axis], axis)


def fold_rows(parts, sub):
    for k in (4, 2, 1):
        half = len(parts) // 2
        first = (sub // k) % 2 == 0
        merged = []
        for i in range(half):
            a, b = parts[i], parts[i + half]
            low = tuple(jnp.where(first, u, roll(v, k, 0)) for u, v in zip(a, b))
            high = tuple(jnp.where(first, roll(u, 8 - k, 0), v) for u, v in zip(a, b))
            merged.append(pair_add(low, high))
        parts = merged
    return parts[0]


def fold_lanes(part):
    for k in (64, 32, 16, 8, 4, 2, 1):
        part = pair_add(part, tuple(roll(v, k, 1) for v in part))
    return norm_pair(part)


def kernel(n_theta, n_ax, a_hbm, j_hbm, g_hbm, w_hbm, out_ref,
           fld, axh, jb, jf, je, gb, wb, early, msg, got0, got1,
           in_sem, send_sem, recv_sem, ar_recv, ready):
    theta, ax = lax.axis_index("theta"), lax.axis_index("ax")
    around = [
        ((theta + n_theta - 1) % n_theta, ax),
        ((theta + 1) % n_theta, ax),
        (theta, (ax + n_ax - 1) % n_ax),
        (theta, (ax + 1) % n_ax),
    ]
    levels = stages(n_theta, n_ax)
    barrier = pltpu.get_barrier_semaphore()
    nz, ny = n_theta // (YL * CORES), (n_ax // X) * YL

    def tell(sem, devices):
        for dev in devices:
            pl.semaphore_signal(sem, inc=1, device_id=dev, device_id_type=MESH)

    rows = [dict(dx=d) for d in range(1, X)]

    def ring(name, size, *distances):
        return [{name: d} for d in sorted({k % size for k in distances} - {0})]

    offsets = rows + [dict(dc=1)] + ring("dy", ny, 1, -1) + ring("dz", nz, 1, -1)
    relays = (
        offsets,
        rows + [dict(dc=1)] + ring("dy", ny, 2, -2) + ring("dz", nz, 2, -2),
        rows + ring("dz", nz, 4, -4),
        [dict(dc=1)],
    )

    def relay(i):
        if i:
            pl.semaphore_wait(ready.at[i - 1], len(relays[i - 1]))
        if i < len(relays):
            tell(ready.at[i], [peer(n_theta, n_ax, **p) for p in relays[i]])

    has = (1, 1, (ax + n_ax - 1) // n_ax, 1 - (ax + 1) // n_ax)
    middle = has[2] * has[3]
    tell(barrier, around[:2])
    for side in (2, 3):
        pl.when(has[side] == 1)(functools.partial(tell, barrier, around[side : side + 1]))
    for level, got in zip(levels, (got0, got1)):
        if len(level) + 1 < got.shape[0]:
            got[len(level) + 1 :] = jnp.zeros((got.shape[0] - len(level) - 1, 128), F32)

    loads = [
        pltpu.make_async_copy(j_hbm, jb, in_sem.at[0]),
        pltpu.make_async_copy(a_hbm, fld.at[0, :, :, 2:6], in_sem.at[1]),
        pltpu.make_async_copy(g_hbm, gb, in_sem.at[1]),
        pltpu.make_async_copy(w_hbm, wb, in_sem.at[1]),
    ]
    for load in loads:
        load.start()
    tell(barrier, [peer(n_theta, n_ax, **p) for p in offsets])
    for side in (0, 1):

        @pl.when(has[2 + side] == 0)
        def _():
            axh[:, side] = jnp.zeros((SWEEPS, OBJ, COMP, NT, 1, 128), F32)

    pl.semaphore_wait(barrier, len(offsets) + 2 + has[2] + has[3])

    sub = lax.broadcasted_iota(jnp.int32, (8, 128), 0)
    lane = lax.broadcasted_iota(jnp.int32, (8, 128), 1)
    sub3 = lax.broadcasted_iota(jnp.int32, (OBJ, 8, 128), 1)

    def await_tiles(sem, like):
        pltpu.make_async_copy(like, like, sem).wait()

    def halo_copies(slot):
        mine = a_hbm if slot == 0 else fld.at[slot, :, :, 2:6]
        moves = (
            (mine.at[:, :, 0:2], fld.at[slot, :, :, 6:8]),
            (mine.at[:, :, 2:4], fld.at[slot, :, :, 0:2]),
            (mine.at[:, :, :, 0:1], axh.at[slot, 1]),
            (mine.at[:, :, :, 7:8], axh.at[slot, 0]),
        )
        return [
            pltpu.make_async_remote_copy(
                src_ref=src, dst_ref=dst, send_sem=send_sem.at[0], recv_sem=recv_sem.at[slot, i // 2],
                device_id=around[i], device_id_type=MESH)
            for i, (src, dst) in enumerate(moves)
        ]

    def theta_part(acc, slot, t, inside):
        for o in range(5):
            if (0 <= t + SHIFT[o] < NT) == inside:
                for m in range(COMP):
                    near = fld[slot, :, m, 2 + t + SHIFT[o]]
                    acc = acc + jf[o, m, :, t][None] * near[:, None]
        return acc

    def local(slot, t):
        acc = -gb[:, :, t] if slot == 0 else jnp.zeros((OBJ, COMP, 8, 128), F32)
        acc = theta_part(acc, slot, t, True)
        for m in range(COMP):
            here = fld[slot, :, m, 2 + t]
            below = jnp.where(sub3 == 0, F32(0.0), pltpu.roll(here, 1, 1))
            above = jnp.where(sub3 == 7, F32(0.0), pltpu.roll(here, 7, 1))
            acc = acc + jf[5, m, :, t][None] * below[:, None]
            acc = acc + jf[6, m, :, t][None] * above[:, None]
        fld[slot + 1, :, :, 2 + t] = acc

    def rest(slot, t):
        acc = fld[slot + 1, :, :, 2 + t]
        for m in range(COMP):
            edge = jnp.where(sub3 < 4, axh[slot, 0, :, m, t], axh[slot, 1, :, m, t])
            acc = acc + je[m, :, t][None] * edge[:, None]
        acc = jnp.where(wb[t] == 1, F32(0.0), acc)
        fld[slot + 1, :, :, 2 + t] = acc
        return acc

    def add_products(sums, values, wanted):
        halves = {s: split(v) for s, v in values.items()}
        sums = list(sums)
        for i, (a, b) in enumerate(wanted):
            p, e = two_prod(values[a], halves[a], values[b], halves[b])
            s, d = two_sum(sums[i][0], p)
            sums[i] = (s, sums[i][1] + (d + e))
        return sums

    zero = jnp.zeros((OBJ, 8, 128), F32)

    def folded(sums):
        parts = [tuple(v[j] for v in s) for s in sums for j in range(OBJ)]
        nothing = jnp.zeros((8, 128), F32)
        return fold_lanes(fold_rows(parts + [(nothing, nothing)] * (8 - len(parts)), sub))

    def early_products(n, sums):
        for t in range(NT):
            values = {s: fld[s, :, n, 2 + t] for s in (1, 2)}
            sums = add_products(sums, values, ((1, 1), (1, 2), (2, 2)))
        return tuple(sums)

    def on_lanes(part, start):
        return (jnp.where(lane == sub + start, part[0], F32(0.0))
                + jnp.where(lane == sub + (start + 8), part[1], F32(0.0)))

    for slot in range(SWEEPS):
        copies = halo_copies(slot)
        for i in (2, 3):
            pl.when(has[i] == 1)(copies[i].start)
        for i in (0, 1):
            copies[i].start()
        relay(slot)
        if slot == 0:
            loads[0].wait()

            def widen(i, carry):
                for m in range(COMP):
                    jf[i, m] = jb[i, m].astype(F32)
                return carry

            lax.fori_loop(0, 7, widen, 0)
            low = jnp.where(sub == 0, F32(1.0), F32(0.0))
            high = jnp.where(sub == 7, F32(1.0), F32(0.0))

            def edges(m, carry):
                je[m] = jf[5, m] * low + jf[6, m] * high
                return carry

            lax.fori_loop(0, COMP, edges, 0)
            for load in loads[1:]:
                load.wait()
        for t in range(NT):
            local(slot, t)
        if slot == 2:
            early[...] = on_lanes(folded(lax.fori_loop(0, COMP, early_products, ((zero, zero),) * 3)), 16)
            relay(3)
        await_tiles(recv_sem.at[slot, 0], je.at[:, 0:4, 0:2])
        for t in range(NT):
            fld[slot + 1, :, :, 2 + t] = theta_part(fld[slot + 1, :, :, 2 + t], slot, t, False)
        pl.when(middle == 1)(functools.partial(await_tiles, recv_sem.at[slot, 1], je.at[:, 0:2, 0:1]))
        pl.when(middle == 0)(functools.partial(await_tiles, recv_sem.at[slot, 1], je.at[:, 0:1, 0:1]))
        sums = [(zero, zero)] * 3
        for t in range(NT):
            acc = rest(slot, t)
            if slot == 2:
                for n in range(COMP):
                    values = {1: fld[1, :, n, 2 + t], 2: fld[2, :, n, 2 + t], 3: acc[:, n]}
                    sums = add_products(sums, values, ((1, 3), (2, 3), (3, 3)))

    row = on_lanes(folded(sums), 0) + early[...]
    for k in (4, 2, 1):
        row = row + roll(row, k, 0)
    is_value = (lane // 8) % 2 == 0
    for i, (level, got) in enumerate(zip(levels, (got0, got1))):
        msg[i] = row
        if i == 1:
            relay(4)
        for k, offset in enumerate(level):
            pltpu.make_async_remote_copy(
                src_ref=msg.at[i, 0:1], dst_ref=got.at[k : k + 1], send_sem=send_sem.at[1],
                recv_sem=ar_recv.at[i], device_id=peer(n_theta, n_ax, **offset), device_id_type=MESH).start()
        got[len(level) : len(level) + 1] = row[0:1]
        heard = got.at[0 : len(level)]
        pltpu.make_async_copy(heard, heard, ar_recv.at[i]).wait()
        sums = [(got[k : k + 8], jnp.zeros((8, 128), F32)) for k in range(0, got.shape[0], 8)]
        while len(sums) > 1:
            paired = [pair_add(a, b) for a, b in zip(sums[0::2], sums[1::2])]
            sums = paired + sums[2 * len(paired):]
        value, error = sums[0]
        for k in (4, 2, 1):
            value, error = pair_add((value, error), (roll(value, k, 0), roll(error, k, 0)))
        value, error = fast_two_sum(value, error + roll(value, -8, 1) + roll(error, -8, 1))
        row = jnp.where(is_value, value, roll(error, 8, 1))

    def gram(start, k):
        place = start + OBJ * k
        return roll(row, -place, 1), roll(row, -place - 8, 1)

    g02, g12, g22 = (gram(0, k) for k in range(3))
    g00, g01, g11 = (gram(16, k) for k in range(3))
    cells = F32(COMP * NT * 8 * 128 * n_theta * n_ax)
    nothing = jnp.zeros((8, 128), F32)

    def step_of(square):
        mean = jnp.maximum(square[0] + square[1], F32(0.0)) / cells
        return F32(STEP) / jnp.sqrt(mean + F32(EPS))

    c0 = step_of(g00)
    p0 = (c0, nothing)
    square1 = pair_add(g00, pair_mul(p0, pair_add(pair_mul(p0, g11), scaled(g01, -2.0))))
    c1 = step_of(square1)
    both = two_sum(c0, c1)
    times = two_prod(c0, split(c0), c1, split(c1))
    inner = pair_add(pair_mul(both, g11), scaled(g01, -2.0))
    outer = pair_add(scaled(pair_add(g02, scaled(pair_mul(both, g12), -1.0)), 2.0), pair_mul(times, g22))
    square2 = pair_add(g00, pair_add(pair_mul(both, inner), pair_mul(times, outer)))
    c2 = step_of(square2)

    def spread(c):
        picked = [jnp.sum(jnp.where(lane == j, c, F32(0.0)), axis=1, keepdims=True) for j in range(OBJ)]
        return jnp.stack([jnp.broadcast_to(v, (8, 128)) for v in picked])[:, None]

    c0, c1, c2 = spread(c0), spread(c1), spread(c2)
    for t in range(NT):
        f0, f1, f2 = (fld[s, :, :, 2 + t] for s in (1, 2, 3))
        r1 = f0 - c0 * f1
        r2 = r1 - c1 * (f1 - c0 * f2)
        out_ref[:, :, t] = c0 * f0 + c1 * r1 + c2 * r2

    pl.when(middle == 1)(functools.partial(await_tiles, send_sem.at[0], jf.at[0:6, :, :, 0:1]))
    pl.when(middle == 0)(functools.partial(await_tiles, send_sem.at[0], jf.at[0:3, 0:3, :, 0:3]))
    for i in range(2):
        heard = (got0, got1)[i].at[0 : len(levels[i])]
        pltpu.make_async_copy(heard, heard, send_sem.at[1]).wait()


def per_device(n_theta, n_ax, adjoint_start, jacobian, objective_gradient, wall_mask):
    field = adjoint_start.shape
    levels = stages(n_theta, n_ax)
    update = pl.pallas_call(
        functools.partial(kernel, n_theta, n_ax),
        out_shape=pltpu.VMEM(field, F32),
        in_specs=[pl.BlockSpec(memory_space=pl.ANY)] * 4,
        out_specs=pl.BlockSpec(memory_space=pltpu.VMEM),
        scratch_shapes=[
            pltpu.VMEM((SWEEPS + 1, OBJ, COMP, NT + 4, 8, 128), F32),
            pltpu.VMEM((SWEEPS, 2, OBJ, COMP, NT, 1, 128), F32),
            pltpu.VMEM(jacobian.shape, jnp.bfloat16),
            pltpu.VMEM(jacobian.shape, F32),
            pltpu.VMEM((COMP, COMP, NT, 8, 128), F32),
            pltpu.VMEM(field, F32),
            pltpu.VMEM(wall_mask.shape, jnp.int32),
            pltpu.VMEM((8, 128), F32),
            pltpu.VMEM((2, 8, 128), F32),
        ]
        + [pltpu.VMEM((rows_of(level), 128), F32) for level in levels]
        + [
            pltpu.SemaphoreType.DMA((2,)),
            pltpu.SemaphoreType.DMA((2,)),
            pltpu.SemaphoreType.DMA((SWEEPS, 2)),
            pltpu.SemaphoreType.DMA((2,)),
            pltpu.SemaphoreType.REGULAR((4,)),
        ],
        compiler_params=pltpu.CompilerParams(collective_id=0, has_side_effects=True),
        name="sweeps",
    )(adjoint_start, jacobian, objective_gradient, wall_mask)
    return adjoint_start - update


def solution(mesh):
    placed = (
        P(None, None, "theta", "ax", None),
        P(None, None, None, "theta", "ax", None),
        P(None, None, "theta", "ax", None),
        P("theta", "ax", None),
    )
    return jax.shard_map(
        functools.partial(per_device, mesh.shape["theta"], mesh.shape["ax"]),
        mesh=mesh,
        in_specs=placed,
        out_specs=P(None, None, "theta", "ax", None),
        check_vma=False,
    )
```

```python
import functools

import jax
import jax.numpy as jnp
from jax import lax
from jax.experimental import pallas as pl
from jax.experimental.pallas import tpu as pltpu
from jax.sharding import PartitionSpec as P

MESH = pl.DeviceIdType.MESH
F32 = jnp.float32
SWEEPS = 3
OBJ = 2
COMP = 5
NT = 4
STEP = 0.4
EPS = 1e-06
SHIFT = (0, -1, 1, -2, 2)

X = 4
YL = 2
CORES = 2


def near_last(size):
    return sorted(range(1, size), key=lambda d: -min(d, size - d))


def peer(n_theta, n_ax, dx=0, dy=0, dz=0, dc=0):
    theta, ax = lax.axis_index("theta"), lax.axis_index("ax")
    nz, ny = n_theta // (YL * CORES), (n_ax // X) * YL
    if dz:
        theta = (theta + YL * CORES * dz) % n_theta
    if dx:
        ax = (ax // X) * X + (ax % X + dx) % X
    if dc:
        theta = (theta // CORES) * CORES + (theta % CORES + dc) % CORES
    if dy:
        y_lo = (theta // CORES) % YL
        y = ((ax // X) * YL + y_lo + dy) % ny
        ax = (y // YL) * X + ax % X
        theta = theta + (y % YL - y_lo) * CORES
    return theta, ax


def stages(n_theta, n_ax):
    nz, ny = n_theta // (YL * CORES), (n_ax // X) * YL
    plane = [(dx, dy) for dx in range(X) for dy in range(ny) if dx or dy]
    plane.sort(key=lambda p: -min(p[0], X - p[0]) - min(p[1], ny - p[1]))
    ring = [(dz, dc) for dz in near_last(nz) + [0] for dc in range(CORES) if dz or dc]
    return (
        [dict(dx=dx, dy=dy) for dx, dy in plane],
        [dict(dz=dz, dc=dc) for dz, dc in ring],
    )


def rows_of(level):
    return -(-(len(level) + 1) // 8) * 8


def two_sum(a, b):
    s = a + b
    bb = s - a
    return s, (a - (s - bb)) + (b - bb)


def fast_two_sum(a, b):
    s = a + b
    return s, b - (s - a)


def split(a):
    c = a * F32(4097.0)
    hi = c - (c - a)
    return hi, a - hi


def two_prod(a, sa, b, sb):
    p = a * b
    return p, ((sa[0] * sb[0] - p) + sa[0] * sb[1] + sa[1] * sb[0]) + sa[1] * sb[1]


def pair_add(a, b):
    s, e = two_sum(a[0], b[0])
    return s, e + (a[1] + b[1])


def norm_pair(a):
    return fast_two_sum(a[0], a[1])


def pair_mul(a, b):
    p, e = two_prod(a[0], split(a[0]), b[0], split(b[0]))
    return fast_two_sum(p, e + (a[0] * b[1] + a[1] * b[0]))


def scaled(a, k):
    return a[0] * F32(k), a[1] * F32(k)


def roll(x, shift, axis):
    return pltpu.roll(x, shift % x.shape[axis], axis)


def fold_rows(parts, sub):
    for k in (4, 2, 1):
        half = len(parts) // 2
        first = (sub // k) % 2 == 0
        merged = []
        for i in range(half):
            a, b = parts[i], parts[i + half]
            low = tuple(jnp.where(first, u, roll(v, k, 0)) for u, v in zip(a, b))
            high = tuple(jnp.where(first, roll(u, 8 - k, 0), v) for u, v in zip(a, b))
            merged.append(pair_add(low, high))
        parts = merged
    return parts[0]


def rolled(part, shift, axis):
    return tuple(roll(v, shift, axis) for v in part)


def fold_four(part, k, axis):
    near = pair_add(part, rolled(part, k, axis))
    return pair_add(near, pair_add(rolled(part, 2 * k, axis), rolled(part, 3 * k, axis)))


def fold_lanes(part):
    for k in (32, 8, 2):
        part = fold_four(part, k, 1)
    return norm_pair(pair_add(part, rolled(part, 1, 1)))


def kernel(n_theta, n_ax, a_hbm, j_hbm, g_hbm, w_hbm, out_ref,
           fld, axh, jb, jf, je, gb, wb, early, msg, got0, got1,
           in_sem, send_sem, recv_sem, ar_recv, ready):
    theta, ax = lax.axis_index("theta"), lax.axis_index("ax")
    around = [
        ((theta + n_theta - 1) % n_theta, ax),
        ((theta + 1) % n_theta, ax),
        (theta, (ax + n_ax - 1) % n_ax),
        (theta, (ax + 1) % n_ax),
    ]
    levels = stages(n_theta, n_ax)
    barrier = pltpu.get_barrier_semaphore()
    nz, ny = n_theta // (YL * CORES), (n_ax // X) * YL

    def tell(sem, devices):
        for dev in devices:
            pl.semaphore_signal(sem, inc=1, device_id=dev, device_id_type=MESH)

    rows = [dict(dx=d) for d in range(1, X)]

    def ring(name, size, *distances):
        return [{name: d} for d in sorted({k % size for k in distances} - {0})]

    offsets = rows + [dict(dc=1)] + ring("dy", ny, 1, -1) + ring("dz", nz, 1, -1)
    relays = (
        offsets,
        rows + [dict(dc=1)] + ring("dy", ny, 2, -2) + ring("dz", nz, 2, -2),
        rows + ring("dz", nz, 4, -4),
        [dict(dc=1)],
    )

    def relay(i):
        if i:
            pl.semaphore_wait(ready.at[i - 1], len(relays[i - 1]))
        if i < len(relays):
            tell(ready.at[i], [peer(n_theta, n_ax, **p) for p in relays[i]])

    has = (1, 1, (ax + n_ax - 1) // n_ax, 1 - (ax + 1) // n_ax)
    middle = has[2] * has[3]
    tell(barrier, around[:2])
    for side in (2, 3):
        pl.when(has[side] == 1)(functools.partial(tell, barrier, around[side : side + 1]))
    for level, got in zip(levels, (got0, got1)):
        if len(level) + 1 < got.shape[0]:
            got[len(level) + 1 :] = jnp.zeros((got.shape[0] - len(level) - 1, 128), F32)

    loads = [
        pltpu.make_async_copy(j_hbm, jb, in_sem.at[0]),
        pltpu.make_async_copy(a_hbm, fld.at[0, :, :, 2:6], in_sem.at[1]),
        pltpu.make_async_copy(g_hbm, gb, in_sem.at[1]),
        pltpu.make_async_copy(w_hbm, wb, in_sem.at[1]),
    ]
    for load in loads:
        load.start()
    tell(barrier, [peer(n_theta, n_ax, **p) for p in offsets])
    for side in (0, 1):

        @pl.when(has[2 + side] == 0)
        def _():
            axh[:, side] = jnp.zeros((SWEEPS, OBJ, COMP, NT, 1, 128), F32)

    pl.semaphore_wait(barrier, len(offsets) + 2 + has[2] + has[3])

    sub = lax.broadcasted_iota(jnp.int32, (8, 128), 0)
    lane = lax.broadcasted_iota(jnp.int32, (8, 128), 1)
    sub3 = lax.broadcasted_iota(jnp.int32, (OBJ, 8, 128), 1)

    def await_tiles(sem, like):
        pltpu.make_async_copy(like, like, sem).wait()

    def halo_copies(slot):
        mine = a_hbm if slot == 0 else fld.at[slot, :, :, 2:6]
        moves = (
            (mine.at[:, :, 0:2], fld.at[slot, :, :, 6:8]),
            (mine.at[:, :, 2:4], fld.at[slot, :, :, 0:2]),
            (mine.at[:, :, :, 0:1], axh.at[slot, 1]),
            (mine.at[:, :, :, 7:8], axh.at[slot, 0]),
        )
        return [
            pltpu.make_async_remote_copy(
                src_ref=src, dst_ref=dst, send_sem=send_sem.at[0], recv_sem=recv_sem.at[slot, i // 2],
                device_id=around[i], device_id_type=MESH)
            for i, (src, dst) in enumerate(moves)
        ]

    def theta_part(acc, slot, t, inside):
        for o in range(5):
            if (0 <= t + SHIFT[o] < NT) == inside:
                for m in range(COMP):
                    near = fld[slot, :, m, 2 + t + SHIFT[o]]
                    acc = acc + jf[o, m, :, t][None] * near[:, None]
        return acc

    def local(slot, t):
        acc = -gb[:, :, t] if slot == 0 else jnp.zeros((OBJ, COMP, 8, 128), F32)
        acc = theta_part(acc, slot, t, True)
        for m in range(COMP):
            here = fld[slot, :, m, 2 + t]
            below = jnp.where(sub3 == 0, F32(0.0), pltpu.roll(here, 1, 1))
            above = jnp.where(sub3 == 7, F32(0.0), pltpu.roll(here, 7, 1))
            acc = acc + jf[5, m, :, t][None] * below[:, None]
            acc = acc + jf[6, m, :, t][None] * above[:, None]
        fld[slot + 1, :, :, 2 + t] = acc

    def rest(slot, t):
        acc = fld[slot + 1, :, :, 2 + t]
        for m in range(COMP):
            edge = jnp.where(sub3 < 4, axh[slot, 0, :, m, t], axh[slot, 1, :, m, t])
            acc = acc + je[m, :, t][None] * edge[:, None]
        acc = jnp.where(wb[t] == 1, F32(0.0), acc)
        fld[slot + 1, :, :, 2 + t] = acc
        return acc

    def add_products(sums, values, wanted):
        halves = {s: split(v) for s, v in values.items()}
        sums = list(sums)
        for i, (a, b) in enumerate(wanted):
            p, e = two_prod(values[a], halves[a], values[b], halves[b])
            s, d = two_sum(sums[i][0], p)
            sums[i] = (s, sums[i][1] + (d + e))
        return sums

    zero = jnp.zeros((OBJ, 8, 128), F32)

    def folded(sums):
        parts = [tuple(v[j] for v in s) for s in sums for j in range(OBJ)]
        nothing = jnp.zeros((8, 128), F32)
        return fold_lanes(fold_rows(parts + [(nothing, nothing)] * (8 - len(parts)), sub))

    def early_products(n, sums):
        for t in range(NT):
            values = {s: fld[s, :, n, 2 + t] for s in (1, 2)}
            sums = add_products(sums, values, ((1, 1), (1, 2), (2, 2)))
        return tuple(sums)

    def on_lanes(part, start):
        return (jnp.where(lane == sub + start, part[0], F32(0.0))
                + jnp.where(lane == sub + (start + 8), part[1], F32(0.0)))

    for slot in range(SWEEPS):
        copies = halo_copies(slot)
        for i in (2, 3):
            pl.when(has[i] == 1)(copies[i].start)
        for i in (0, 1):
            copies[i].start()
        relay(slot)
        if slot == 0:
            loads[0].wait()

            def widen(i, carry):
                for m in range(COMP):
                    jf[i, m] = jb[i, m].astype(F32)
                return carry

            lax.fori_loop(0, 7, widen, 0)
            low = jnp.where(sub == 0, F32(1.0), F32(0.0))
            high = jnp.where(sub == 7, F32(1.0), F32(0.0))

            def edges(m, carry):
                je[m] = jf[5, m] * low + jf[6, m] * high
                return carry

            lax.fori_loop(0, COMP, edges, 0)
            for load in loads[1:]:
                load.wait()
        for t in range(NT):
            local(slot, t)
        if slot == 2:
            early[...] = on_lanes(folded(lax.fori_loop(0, COMP, early_products, ((zero, zero),) * 3)), 16)
            relay(3)
        await_tiles(recv_sem.at[slot, 0], je.at[:, 0:4, 0:2])
        for t in range(NT):
            fld[slot + 1, :, :, 2 + t] = theta_part(fld[slot + 1, :, :, 2 + t], slot, t, False)
        pl.when(middle == 1)(functools.partial(await_tiles, recv_sem.at[slot, 1], je.at[:, 0:2, 0:1]))
        pl.when(middle == 0)(functools.partial(await_tiles, recv_sem.at[slot, 1], je.at[:, 0:1, 0:1]))
        sums = [(zero, zero)] * 3
        for t in range(NT):
            acc = rest(slot, t)
            if slot == 2:
                for n in range(COMP):
                    values = {1: fld[1, :, n, 2 + t], 2: fld[2, :, n, 2 + t], 3: acc[:, n]}
                    sums = add_products(sums, values, ((1, 3), (2, 3), (3, 3)))

    row = on_lanes(folded(sums), 0) + early[...]
    for k in (4, 2, 1):
        row = row + roll(row, k, 0)
    is_value = (lane // 8) % 2 == 0
    for i, (level, got) in enumerate(zip(levels, (got0, got1))):
        msg[i] = row
        if i == 1:
            relay(4)
        for k, offset in enumerate(level):
            pltpu.make_async_remote_copy(
                src_ref=msg.at[i, 0:1], dst_ref=got.at[k : k + 1], send_sem=send_sem.at[1],
                recv_sem=ar_recv.at[i], device_id=peer(n_theta, n_ax, **offset), device_id_type=MESH).start()
        got[len(level) : len(level) + 1] = row[0:1]
        heard = got.at[0 : len(level)]
        pltpu.make_async_copy(heard, heard, ar_recv.at[i]).wait()
        sums = [(got[k : k + 8], jnp.zeros((8, 128), F32)) for k in range(0, got.shape[0], 8)]
        while len(sums) > 1:
            paired = [pair_add(a, b) for a, b in zip(sums[0::2], sums[1::2])]
            sums = paired + sums[2 * len(paired):]
        value, error = sums[0]
        value, error = fold_four((value, error), 2, 0)
        value, error = pair_add((value, error), (roll(value, 1, 0), roll(error, 1, 0)))
        value, error = fast_two_sum(value, error + roll(value, -8, 1) + roll(error, -8, 1))
        row = jnp.where(is_value, value, roll(error, 8, 1))

    def gram(start, k):
        place = start + OBJ * k
        return roll(row, -place, 1), roll(row, -place - 8, 1)

    g02, g12, g22 = (gram(0, k) for k in range(3))
    g00, g01, g11 = (gram(16, k) for k in range(3))
    cells = F32(COMP * NT * 8 * 128 * n_theta * n_ax)
    nothing = jnp.zeros((8, 128), F32)

    def step_of(square):
        mean = jnp.maximum(square[0] + square[1], F32(0.0)) / cells
        return F32(STEP) / jnp.sqrt(mean + F32(EPS))

    c0 = step_of(g00)
    p0 = (c0, nothing)
    square1 = pair_add(g00, pair_mul(p0, pair_add(pair_mul(p0, g11), scaled(g01, -2.0))))
    c1 = step_of(square1)
    both = two_sum(c0, c1)
    times = two_prod(c0, split(c0), c1, split(c1))
    inner = pair_add(pair_mul(both, g11), scaled(g01, -2.0))
    outer = pair_add(scaled(pair_add(g02, scaled(pair_mul(both, g12), -1.0)), 2.0), pair_mul(times, g22))
    square2 = pair_add(g00, pair_add(pair_mul(both, inner), pair_mul(times, outer)))
    c2 = step_of(square2)

    def spread(c):
        picked = [jnp.sum(jnp.where(lane == j, c, F32(0.0)), axis=1, keepdims=True) for j in range(OBJ)]
        return jnp.stack([jnp.broadcast_to(v, (8, 128)) for v in picked])[:, None]

    c0, c1, c2 = spread(c0), spread(c1), spread(c2)
    for t in range(NT):
        f0, f1, f2 = (fld[s, :, :, 2 + t] for s in (1, 2, 3))
        r1 = f0 - c0 * f1
        r2 = r1 - c1 * (f1 - c0 * f2)
        out_ref[:, :, t] = c0 * f0 + c1 * r1 + c2 * r2

    pl.when(middle == 1)(functools.partial(await_tiles, send_sem.at[0], jf.at[0:6, :, :, 0:1]))
    pl.when(middle == 0)(functools.partial(await_tiles, send_sem.at[0], jf.at[0:3, 0:3, :, 0:3]))
    for i in range(2):
        heard = (got0, got1)[i].at[0 : len(levels[i])]
        pltpu.make_async_copy(heard, heard, send_sem.at[1]).wait()


def per_device(n_theta, n_ax, adjoint_start, jacobian, objective_gradient, wall_mask):
    field = adjoint_start.shape
    levels = stages(n_theta, n_ax)
    update = pl.pallas_call(
        functools.partial(kernel, n_theta, n_ax),
        out_shape=pltpu.VMEM(field, F32),
        in_specs=[pl.BlockSpec(memory_space=pl.ANY)] * 4,
        out_specs=pl.BlockSpec(memory_space=pltpu.VMEM),
        scratch_shapes=[
            pltpu.VMEM((SWEEPS + 1, OBJ, COMP, NT + 4, 8, 128), F32),
            pltpu.VMEM((SWEEPS, 2, OBJ, COMP, NT, 1, 128), F32),
            pltpu.VMEM(jacobian.shape, jnp.bfloat16),
            pltpu.VMEM(jacobian.shape, F32),
            pltpu.VMEM((COMP, COMP, NT, 8, 128), F32),
            pltpu.VMEM(field, F32),
            pltpu.VMEM(wall_mask.shape, jnp.int32),
            pltpu.VMEM((8, 128), F32),
            pltpu.VMEM((2, 8, 128), F32),
        ]
        + [pltpu.VMEM((rows_of(level), 128), F32) for level in levels]
        + [
            pltpu.SemaphoreType.DMA((2,)),
            pltpu.SemaphoreType.DMA((2,)),
            pltpu.SemaphoreType.DMA((SWEEPS, 2)),
            pltpu.SemaphoreType.DMA((2,)),
            pltpu.SemaphoreType.REGULAR((4,)),
        ],
        compiler_params=pltpu.CompilerParams(collective_id=0, has_side_effects=True),
        name="sweeps",
    )(adjoint_start, jacobian, objective_gradient, wall_mask)
    return adjoint_start - update


def solution(mesh):
    placed = (
        P(None, None, "theta", "ax", None),
        P(None, None, None, "theta", "ax", None),
        P(None, None, "theta", "ax", None),
        P("theta", "ax", None),
    )
    return jax.shard_map(
        functools.partial(per_device, mesh.shape["theta"], mesh.shape["ax"]),
        mesh=mesh,
        in_specs=placed,
        out_specs=P(None, None, "theta", "ax", None),
        check_vma=False,
    )
```
